256 devices in a mesh: panel: 8 (over x, y_hi), leaf: 32 (over y_lo, z, core).
Axes of the slice: x: 4, y: 4 (y_hi: 2, y_lo: 2; y = y_hi * 2 + y_lo), z: 8, core: 2. Of those that a mesh axis runs over, the one named last changes fastest.
Arguments:
- excitation: bfloat16 [2, 128, 786432], P(None, None, ('panel', 'leaf')), may hold values from -6 to 6
- point_order: int32 [256, 3072], P(('panel', 'leaf')), may hold values from 0 to 3071, each once within a row
- projection: bfloat16 [2, 256, 786432], P(None, None, ('panel', 'leaf')), may hold values from -0.078125 to 0.078125
- transfer: bfloat16 [5, 2, 65536, 512], P(None, None, ('panel', 'leaf')), may hold values from -0.1875 to 0.1875
- expansion: bfloat16 [2, 256, 786432], P(None, None, ('panel', 'leaf')), may hold values from -0.09375 to 0.09375
Outputs:
- response: bfloat16 [2, 128, 786432], P(None, None, ('panel', 'leaf'))
The draws below stay inside these ranges and needn't reach their ends.
Inputs may be any that keep to these rules, and one draw needn't show every extreme that they name: Each row of point_order holds every number of 0 to 3071 once.
All inputs are finite; a program needn't handle non-finite values.
Results may differ from the reference program's by a relative error of at most 0.018.
Values may be sent and summed in bfloat16 or wider, within the bound.
No kernel may reach another device: no remote copies, remote signals or barrier semaphores. Data moves between devices by JAX's collectives and lax.ppermute only.
A program may use at most 64 MiB of HBM per device.

```python
import jax
import jax.numpy as jnp
from jax import lax

R = 256
EXC = 128
ROWS = 3072
LEVELS = 5
N = 786432
N_PANEL = 8
N_LEAF = 32


def shard_levels(key, extent, shards, low, top_value):
    level = 1.0
    for axis_at, parts in shards:
        steps = jax.random.uniform(jax.random.fold_in(jax.random.fold_in(key, 6), axis_at), (parts,), jnp.float32, low / len(shards), top_value / len(shards))
        level = level * jnp.repeat(jnp.exp(steps), extent[axis_at] // parts).reshape((-1,) + (1,) * (len(extent) - 1 - axis_at))
    return level


def bell_draw(rng, dims, spread, bound, split=(), held_as=jnp.bfloat16):
    drawn = spread * jax.random.normal(rng, dims, jnp.float32)
    if split:
        drawn = drawn * shard_levels(rng, dims, split, -0.22, 0.18)
    return jnp.clip(drawn, -bound, bound).astype(held_as)


def setup_inputs(seed: int = 0) -> dict:
    key_of = jax.random.split(jax.random.key(seed), 6)
    excitation = bell_draw(key_of[0], (2, EXC, N), 1.0, 6.0, ((2, 256),))
    point_order = jax.vmap(lambda own: jax.random.permutation(own, ROWS))(jax.random.split(key_of[1], (N_PANEL * N_LEAF))).reshape((N_PANEL * N_LEAF, ROWS)).astype(jnp.int32)
    projection = bell_draw(key_of[2], (2, R, N), (2 * ROWS) ** -0.5, 0.078125, ((2, 256),))
    transfer = bell_draw(key_of[3], (LEVELS, 2, N_PANEL * N_LEAF * R, 2 * R), (4 * R) ** -0.5, 0.1875, ((2, 256),))
    expansion = bell_draw(key_of[4], (2, R, N), (2 * R * N_PANEL) ** -0.5, 0.09375, ((2, 256),))
    return dict(excitation=excitation, point_order=point_order, projection=projection, transfer=transfer, expansion=expansion)


def complex_dot(first_matrix, second_matrix, first_dim, second_dim):
    contract = (((first_dim,), (second_dim,)), ((), ()))

    def real_dot(first_part, second_part):
        return lax.dot_general(first_part, second_part, contract, preferred_element_type=jnp.float32)

    real_part = real_dot(first_matrix[0], second_matrix[0]) - real_dot(first_matrix[1], second_matrix[1])
    imag_part = real_dot(first_matrix[0], second_matrix[1]) + real_dot(first_matrix[1], second_matrix[0])
    return jnp.stack((real_part, imag_part))


def complex_einsum(form, first_matrix, second_matrix):
    first_wide = first_matrix.astype(jnp.float32)
    second_wide = second_matrix.astype(jnp.float32)
    real_part = jnp.einsum(form, first_wide[0], second_wide[0]) - jnp.einsum(form, first_wide[1], second_wide[1])
    imag_part = jnp.einsum(form, first_wide[0], second_wide[1]) + jnp.einsum(form, first_wide[1], second_wide[0])
    return jnp.stack((real_part, imag_part))


def reference(excitation, point_order, projection, transfer, expansion):
    node_count = N_PANEL * N_LEAF
    reshaped = excitation.reshape(2, EXC, node_count, ROWS)

    def project(block_index):
        block_values = lax.dynamic_index_in_dim(reshaped, block_index, 2, keepdims=False)
        order_row = lax.dynamic_index_in_dim(point_order, block_index, 0, keepdims=False)
        ordered = jnp.take(block_values, order_row, axis=2)
        basis = lax.dynamic_slice_in_dim(projection, (block_index * ROWS).astype(jnp.int32), ROWS, 2)
        return complex_dot(basis, ordered, 1, 1).astype(jnp.bfloat16)

    blocks_coeff = lax.map(project, jnp.arange(node_count, dtype=jnp.int32))
    coefficients = jnp.transpose(blocks_coeff, (1, 0, 2, 3)).reshape(2, N_PANEL, N_LEAF, R, EXC)
    for level in range(LEVELS):
        span = 2 ** level
        grouped = coefficients.reshape(2, N_PANEL, N_LEAF // (2 * span), 2, span, R, EXC)
        lower_side = jnp.broadcast_to(grouped[:, :, :, 0:1], grouped.shape).reshape(coefficients.shape)
        upper_side = jnp.broadcast_to(grouped[:, :, :, 1:2], grouped.shape).reshape(coefficients.shape)
        matrices = transfer[level].reshape(2, N_PANEL, N_LEAF, R, 2 * R)
        mixed_sum = complex_einsum("pnrk,pnke->pnre", matrices[..., :R], lower_side)
        mixed_sum = mixed_sum + complex_einsum("pnrk,pnke->pnre", matrices[..., R:], upper_side)
        coefficients = mixed_sum.astype(jnp.bfloat16)
    total = jnp.sum(coefficients.astype(jnp.float32), axis=1).astype(jnp.bfloat16)

    def expand(panel_index):
        start_col = (panel_index * N_LEAF * ROWS).astype(jnp.int32)
        basis = lax.dynamic_slice_in_dim(expansion, start_col, N_LEAF * ROWS, 2).reshape(2, R, N_LEAF, ROWS)
        return complex_einsum("ike,kir->eir", total, basis)

    expanded = lax.map(expand, jnp.arange(N_PANEL, dtype=jnp.int32))
    response = jnp.transpose(expanded, (1, 2, 0, 3, 4)).reshape(2, EXC, N)
    return response.astype(jnp.bfloat16)
```

```python
import functools

import jax
import jax.numpy as jnp
from jax import lax
from jax.experimental import pallas as pl
from jax.experimental.pallas import tpu as pltpu
from jax.sharding import PartitionSpec as P


def partner_2(block, axis, stride):
    count = lax.axis_size(axis)
    route = []
    for low in range(count):
        high = low | 1 << stride
        if high != low and high < count:
            route += [(low, high), (high, low)]
    return lax.ppermute(block, axis, route)


def copy_for_each(x, axis):
    count = lax.axis_size(axis)
    return lax.all_to_all(jnp.broadcast_to(x[None], (count, *x.shape)), axis, 0, 0, tiled=True)


def taken_together(x, axis):
    return copy_for_each(x, axis).astype(jnp.float32).sum(axis=0)


def complex_dot(first_matrix, second_matrix, first_dim, second_dim):
    contract = (((first_dim,), (second_dim,)), ((), ()))

    def real_dot(first_part, second_part):
        return lax.dot_general(
            first_part, second_part, contract, preferred_element_type=jnp.float32
        )

    real_part = real_dot(first_matrix[0], second_matrix[0]) - real_dot(
        first_matrix[1], second_matrix[1]
    )
    imag_part = real_dot(first_matrix[0], second_matrix[1]) + real_dot(
        first_matrix[1], second_matrix[0]
    )
    return jnp.stack((real_part, imag_part))


def leaf_kernel(order_ref, source_ref, basis_ref, out_ref, total_ref):
    _, width, points = source_ref.shape
    rank, chunk = basis_ref.shape[1:]
    step = pl.program_id(0)
    source = source_ref[...].reshape(2 * width, points)
    point = lax.broadcasted_iota(jnp.int16, (points, chunk), 0)
    chosen = jnp.where(
        point == order_ref[...].astype(jnp.int16), jnp.bfloat16(1), jnp.bfloat16(0)
    )
    ordered = jnp.dot(source, chosen, preferred_element_type=jnp.float32).astype(jnp.bfloat16)
    basis = basis_ref[...].reshape(2 * rank, chunk)
    product = lax.dot_general(
        basis, ordered, (((1,), (1,)), ((), ())), preferred_element_type=jnp.float32
    )

    @pl.when(step == 0)
    def _():
        total_ref[...] = product

    @pl.when(step > 0)
    def _():
        total_ref[...] += product

    @pl.when(step == pl.num_programs(0) - 1)
    def _():
        total = total_ref[...]
        out_ref[0] = (total[:rank, :width] - total[rank:, width:]).astype(jnp.bfloat16)
        out_ref[1] = (total[:rank, width:] + total[rank:, :width]).astype(jnp.bfloat16)


def leaf_coefficients(excitation, point_order, projection, chunk=512):
    _, width, points = excitation.shape
    rank = projection.shape[1]
    return pl.pallas_call(
        leaf_kernel,
        grid=(points // chunk,),
        in_specs=[
            pl.BlockSpec((1, chunk), lambda j: (0, j)),
            pl.BlockSpec((2, width, points), lambda j: (0, 0, 0)),
            pl.BlockSpec((2, rank, chunk), lambda j: (0, 0, j)),
        ],
        out_specs=pl.BlockSpec((2, rank, width), lambda j: (0, 0, 0)),
        out_shape=jax.ShapeDtypeStruct((2, rank, width), jnp.bfloat16),
        scratch_shapes=[pltpu.VMEM((2 * rank, 2 * width), jnp.float32)],
        name="leaf",
    )(point_order, excitation, projection)


def per_device(excitation, point_order, projection, transfer, expansion):
    coefficients = leaf_coefficients(excitation, point_order, projection)
    position = lax.axis_index("leaf")
    rank_width = coefficients.shape[1]
    for level in range(lax.axis_size("leaf").bit_length() - 1):
        partner = partner_2(coefficients, "leaf", level)
        upper_bit = position >> level & 1 == 1
        matrix = transfer[level]
        first_block = matrix[:, :, :rank_width]
        second_block = matrix[:, :, rank_width:]
        own_matrix = jnp.where(upper_bit, second_block, first_block)
        other_matrix = jnp.where(upper_bit, first_block, second_block)
        own_term = complex_dot(own_matrix, coefficients, 1, 0)
        partner_term = complex_dot(other_matrix, partner, 1, 0)
        coefficients = (own_term + partner_term).astype(jnp.bfloat16)
    summed = taken_together(coefficients, "panel").astype(jnp.bfloat16)
    result = complex_dot(summed, expansion, 0, 0)
    return result.astype(jnp.bfloat16)


def solution(mesh):
    in_specs = (
        P(None, None, ("panel", "leaf")),
        P(("panel", "leaf"), None),
        P(None, None, ("panel", "leaf")),
        P(None, None, ("panel", "leaf"), None),
        P(None, None, ("panel", "leaf")),
    )
    out_specs = P(None, None, ("panel", "leaf"))
    return jax.shard_map(
        per_device, mesh=mesh, in_specs=in_specs, out_specs=out_specs, check_vma=False
    )
```

```python
import functools

import jax
import jax.numpy as jnp
from jax import lax
from jax.experimental import pallas as pl
from jax.experimental.pallas import tpu as pltpu
from jax.sharding import PartitionSpec as P


def swap(block, axis, mask):
    count = lax.axis_size(axis)
    return lax.ppermute(block, axis, [(place, place ^ mask) for place in range(count)])


def leaf_kernel(order_hbm, source_hbm, basis_hbm, out_ref, order_ref, source_ref, basis_ref, by_point_ref, *rest):
    ordered_refs, (order_done, source_done, basis_done) = rest[:-3], rest[-3:]
    _, width, points = source_ref.shape
    rank = basis_ref.shape[1]
    chunk = ordered_refs[0].shape[0] // 2
    order_copy = pltpu.make_async_copy(order_hbm, order_ref, order_done)
    source_copies = [
        pltpu.make_async_copy(source_hbm.at[part], source_ref.at[part], source_done.at[part])
        for part in range(2)
    ]
    basis_copies = [
        pltpu.make_async_copy(basis_hbm.at[part], basis_ref.at[part], basis_done.at[part])
        for part in range(2)
    ]
    for copy in (order_copy, *source_copies, *basis_copies):
        copy.start()
    for part in range(2):
        source_copies[part].wait()
        for start in range(0, points, 256):
            block = source_ref[part, :, start : start + 256].astype(jnp.float32)
            by_point_ref[pl.ds(2 * start + part, 256, stride=2), :] = block.T
    order_copy.wait()
    total = None
    for at in range(len(ordered_refs) + 1):
        if at == 1:
            for copy in basis_copies:
                copy.wait()
        if at < len(ordered_refs):
            for row in range(chunk):
                point = pl.multiple_of(2 * order_ref[0, at * chunk + row], 2)
                ordered_refs[at][2 * row : 2 * row + 2, :] = by_point_ref[pl.ds(point, 2), :]
        if at > 0:
            ordered = jnp.concatenate(
                [
                    ordered_refs[at - 1][pl.ds(part, chunk, stride=2), :].astype(jnp.bfloat16)
                    for part in range(2)
                ],
                axis=1,
            )
            basis = basis_ref[:, :, (at - 1) * chunk : at * chunk].reshape(2 * rank, chunk)
            term = jnp.dot(basis, ordered, preferred_element_type=jnp.float32)
            total = term if total is None else total + term
    out_ref[:rank] = (total[:rank, :width] - total[rank:, width:]).astype(jnp.bfloat16)
    out_ref[rank:] = (total[:rank, width:] + total[rank:, :width]).astype(jnp.bfloat16)


def leaf_coefficients(excitation, point_order, projection, chunk=512):
    _, width, points = excitation.shape
    rank = projection.shape[1]
    point_order, excitation, projection = (
        pltpu.with_memory_space_constraint(array, pltpu.HBM)
        for array in (point_order, excitation, projection)
    )
    return pl.pallas_call(
        leaf_kernel,
        in_specs=[pl.BlockSpec(memory_space=pltpu.HBM)] * 3,
        out_specs=pl.BlockSpec(memory_space=pltpu.VMEM),
        out_shape=jax.ShapeDtypeStruct((2 * rank, width), jnp.bfloat16),
        scratch_shapes=[
            pltpu.SMEM((1, points), jnp.int32),
            pltpu.VMEM(excitation.shape, jnp.bfloat16),
            pltpu.VMEM(projection.shape, jnp.bfloat16),
            pltpu.VMEM((2 * points, width), jnp.float32),
            *[pltpu.VMEM((2 * chunk, width), jnp.float32)] * (points // chunk),
            pltpu.SemaphoreType.DMA,
            pltpu.SemaphoreType.DMA((2,)),
            pltpu.SemaphoreType.DMA((2,)),
        ],
        compiler_params=pltpu.CompilerParams(vmem_limit_bytes=24 << 20),
        name="leaf",
    )(point_order, excitation, projection)


def expand_kernel(total_ref, basis_ref, out_hbm, left_ref, out_ref, done):
    rank, points = basis_ref.shape[1:]
    width = total_ref.shape[1]
    chunk = points // done.shape[0]
    left_ref[:width] = total_ref[:rank].T
    left_ref[width:] = total_ref[rank:].T
    left = left_ref[...]
    copies = []
    for at in range(points // chunk):
        here = pl.ds(at * chunk, chunk)
        by_real = jnp.dot(left, basis_ref[0, :, here], preferred_element_type=jnp.float32)
        by_imag = jnp.dot(left, basis_ref[1, :, here], preferred_element_type=jnp.float32)
        out_ref[0, :, here] = (by_real[:width] - by_imag[width:]).astype(jnp.bfloat16)
        out_ref[1, :, here] = (by_real[width:] + by_imag[:width]).astype(jnp.bfloat16)
        copies.append(
            pltpu.make_async_copy(out_ref.at[:, :, here], out_hbm.at[:, :, here], done.at[at])
        )
        copies[-1].start()
    for copy in copies:
        copy.wait()


def expanded(total, expansion, chunk=512):
    _, rank, points = expansion.shape
    width = total.shape[1]
    return pl.pallas_call(
        expand_kernel,
        in_specs=[pl.BlockSpec(memory_space=pltpu.VMEM)] * 2,
        out_specs=pl.BlockSpec(memory_space=pltpu.HBM),
        out_shape=jax.ShapeDtypeStruct((2, width, points), jnp.bfloat16),
        scratch_shapes=[
            pltpu.VMEM((2 * width, rank), jnp.bfloat16),
            pltpu.VMEM((2, width, points), jnp.bfloat16),
            pltpu.SemaphoreType.DMA((points // chunk,)),
        ],
        compiler_params=pltpu.CompilerParams(vmem_limit_bytes=16 << 20),
        name="expand",
    )(total, expansion)


def level_kernel(coefficients_ref, matrix_ref, own_ref, other_ref, *, level):
    rank = matrix_ref.shape[2]
    width = coefficients_ref.shape[1]
    upper = lax.axis_index("leaf") >> level & 1
    own_half = pl.ds(pl.multiple_of(upper * rank, rank), rank)
    other_half = pl.ds(pl.multiple_of((1 - upper) * rank, rank), rank)
    matrix = matrix_ref[0, :, :, own_half].reshape(2 * rank, rank)
    coefficients = jnp.concatenate(
        (coefficients_ref[:rank], coefficients_ref[rank:]), axis=1
    )
    term = jnp.dot(matrix, coefficients, preferred_element_type=jnp.float32)
    own_ref[:rank] = term[:rank, :width] - term[rank:, width:]
    own_ref[rank:] = term[:rank, width:] + term[rank:, :width]
    real = matrix_ref[0, 0, :, other_half]
    imag = matrix_ref[0, 1, :, other_half]
    other_ref[:rank, :rank] = real
    other_ref[:rank, rank:] = -imag
    other_ref[rank:, :rank] = imag
    other_ref[rank:, rank:] = real


def own_part(coefficients, transfer, level):
    rank = transfer.shape[2]
    whole = lambda _: (0, 0)
    return pl.pallas_call(
        functools.partial(level_kernel, level=level),
        grid=(1,),
        in_specs=[
            pl.BlockSpec(coefficients.shape, whole),
            pl.BlockSpec((1, 2, rank, 2 * rank), lambda _: (level, 0, 0, 0)),
        ],
        out_specs=[
            pl.BlockSpec(coefficients.shape, whole),
            pl.BlockSpec((2 * rank, 2 * rank), whole),
        ],
        out_shape=[
            jax.ShapeDtypeStruct(coefficients.shape, jnp.float32),
            jax.ShapeDtypeStruct((2 * rank, 2 * rank), jnp.bfloat16),
        ],
        compiler_params=pltpu.CompilerParams(vmem_limit_bytes=8 << 20),
        cost_estimate=pl.CostEstimate(
            flops=8 * rank * rank * coefficients.shape[1],
            bytes_accessed=8 * rank * rank * 2,
            transcendentals=0,
        ),
        name="own_part",
    )(coefficients, transfer)


def per_device(excitation, point_order, projection, transfer, expansion):
    coefficients = leaf_coefficients(excitation, point_order, projection)
    for level in range(transfer.shape[0]):
        partner = swap(coefficients, "leaf", 1 << level)
        own_term, other = own_part(coefficients, transfer, level)
        other_term = jnp.dot(other, partner, preferred_element_type=jnp.float32)
        coefficients = (own_term + other_term).astype(jnp.bfloat16)
    pair = swap(coefficients, "panel", 1)
    coefficients = (coefficients.astype(jnp.float32) + pair.astype(jnp.float32)).astype(jnp.bfloat16)
    across = [swap(coefficients, "panel", mask) for mask in (4, 2, 6)]
    total = coefficients.astype(jnp.float32)
    for term in across:
        total = total + term.astype(jnp.float32)
    return expanded(total.astype(jnp.bfloat16), expansion)


def solution(mesh):
    in_specs = (
        P(None, None, ("panel", "leaf")),
        P(("panel", "leaf"), None),
        P(None, None, ("panel", "leaf")),
        P(None, None, ("panel", "leaf"), None),
        P(None, None, ("panel", "leaf")),
    )
    out_specs = P(None, None, ("panel", "leaf"))
    return jax.shard_map(
        per_device, mesh=mesh, in_specs=in_specs, out_specs=out_specs, check_vma=False
    )
```

```python
import functools

import jax
import jax.numpy as jnp
from jax import lax
from jax.experimental import pallas as pl
from jax.experimental.pallas import tpu as pltpu
from jax.sharding import PartitionSpec as P


def swap(block, axis, mask):
    count = lax.axis_size(axis)
    return lax.ppermute(block, axis, [(place, place ^ mask) for place in range(count)])


def leaf_kernel(order_hbm, source_hbm, basis_hbm, out_ref, order_ref, source_ref, basis_ref, by_point_ref, *rest):
    ordered_refs, (order_done, source_done, basis_done) = rest[:-3], rest[-3:]
    _, width, points = source_ref.shape
    rank = basis_ref.shape[1]
    chunk = ordered_refs[0].shape[0] // 2
    order_copy = pltpu.make_async_copy(order_hbm, order_ref, order_done)
    source_copies = [
        pltpu.make_async_copy(source_hbm.at[part], source_ref.at[part], source_done.at[part])
        for part in range(2)
    ]
    basis_copies = [
        pltpu.make_async_copy(basis_hbm.at[part], basis_ref.at[part], basis_done.at[part])
        for part in range(2)
    ]
    for copy in (order_copy, *source_copies, *basis_copies):
        copy.start()
    for part in range(2):
        source_copies[part].wait()
        for start in range(0, points, 256):
            block = source_ref[part, :, start : start + 256].astype(jnp.float32)
            by_point_ref[pl.ds(2 * start + part, 256, stride=2), :] = block.T
    order_copy.wait()
    total = None
    for at in range(len(ordered_refs) + 1):
        if at == 1:
            for copy in basis_copies:
                copy.wait()
        if at < len(ordered_refs):
            for row in range(chunk):
                point = pl.multiple_of(2 * order_ref[0, at * chunk + row], 2)
                ordered_refs[at][2 * row : 2 * row + 2, :] = by_point_ref[pl.ds(point, 2), :]
        if at > 0:
            ordered = jnp.concatenate(
                [
                    ordered_refs[at - 1][pl.ds(part, chunk, stride=2), :].astype(jnp.bfloat16)
                    for part in range(2)
                ],
                axis=1,
            )
            basis = basis_ref[:, :, (at - 1) * chunk : at * chunk].reshape(2 * rank, chunk)
            term = jnp.dot(basis, ordered, preferred_element_type=jnp.float32)
            total = term if total is None else total + term
    out_ref[:rank] = (total[:rank, :width] - total[rank:, width:]).astype(jnp.bfloat16)
    out_ref[rank:] = (total[:rank, width:] + total[rank:, :width]).astype(jnp.bfloat16)


def leaf_coefficients(excitation, point_order, projection, chunk=512):
    _, width, points = excitation.shape
    rank = projection.shape[1]
    point_order, excitation, projection = (
        pltpu.with_memory_space_constraint(array, pltpu.HBM)
        for array in (point_order, excitation, projection)
    )
    return pl.pallas_call(
        leaf_kernel,
        in_specs=[pl.BlockSpec(memory_space=pltpu.HBM)] * 3,
        out_specs=pl.BlockSpec(memory_space=pltpu.VMEM),
        out_shape=jax.ShapeDtypeStruct((2 * rank, width), jnp.bfloat16),
        scratch_shapes=[
            pltpu.SMEM((1, points), jnp.int32),
            pltpu.VMEM(excitation.shape, jnp.bfloat16),
            pltpu.VMEM(projection.shape, jnp.bfloat16),
            pltpu.VMEM((2 * points, width), jnp.float32),
            *[pltpu.VMEM((2 * chunk, width), jnp.float32)] * (points // chunk),
            pltpu.SemaphoreType.DMA,
            pltpu.SemaphoreType.DMA((2,)),
            pltpu.SemaphoreType.DMA((2,)),
        ],
        compiler_params=pltpu.CompilerParams(vmem_limit_bytes=24 << 20),
        name="leaf",
    )(point_order, excitation, projection)


def expand_kernel(total_ref, basis_ref, out_hbm, left_ref, out_ref, done):
    rank, points = basis_ref.shape[1:]
    width = total_ref.shape[1]
    chunk = points // done.shape[0]
    left_ref[:width] = total_ref[:rank].T
    left_ref[width:] = total_ref[rank:].T
    left = left_ref[...]
    copies = []
    for at in range(points // chunk):
        here = pl.ds(at * chunk, chunk)
        by_real = jnp.dot(left, basis_ref[0, :, here], preferred_element_type=jnp.float32)
        by_imag = jnp.dot(left, basis_ref[1, :, here], preferred_element_type=jnp.float32)
        out_ref[0, :, here] = (by_real[:width] - by_imag[width:]).astype(jnp.bfloat16)
        out_ref[1, :, here] = (by_real[width:] + by_imag[:width]).astype(jnp.bfloat16)
        copies.append(
            pltpu.make_async_copy(out_ref.at[:, :, here], out_hbm.at[:, :, here], done.at[at])
        )
        copies[-1].start()
    for copy in copies:
        copy.wait()


def expanded(total, expansion, chunk=512):
    _, rank, points = expansion.shape
    width = total.shape[1]
    return pl.pallas_call(
        expand_kernel,
        in_specs=[pl.BlockSpec(memory_space=pltpu.VMEM)] * 2,
        out_specs=pl.BlockSpec(memory_space=pltpu.HBM),
        out_shape=jax.ShapeDtypeStruct((2, width, points), jnp.bfloat16),
        scratch_shapes=[
            pltpu.VMEM((2 * width, rank), jnp.bfloat16),
            pltpu.VMEM((2, width, points), jnp.bfloat16),
            pltpu.SemaphoreType.DMA((points // chunk,)),
        ],
        compiler_params=pltpu.CompilerParams(vmem_limit_bytes=16 << 20),
        name="expand",
    )(total, expansion)


def half_of(transfer_ref, level, own):
    rank = transfer_ref.shape[2]
    upper = lax.axis_index("leaf") >> level & 1
    side = upper if own else 1 - upper
    return transfer_ref[level, :, :, pl.ds(pl.multiple_of(side * rank, rank), rank)]


def complex_product(matrix, coefficients):
    _, rows, rank = matrix.shape
    width = coefficients.shape[1]
    side_by_side = jnp.concatenate((coefficients[:rank], coefficients[rank:]), axis=1)
    term = jnp.dot(
        matrix.reshape(2 * rows, rank), side_by_side, preferred_element_type=jnp.float32
    )
    return term[:rows, :width] - term[rows:, width:], term[:rows, width:] + term[rows:, :width]


def put(out_ref, parts):
    rank = out_ref.shape[0] // 2
    out_ref[:rank] = parts[0].astype(out_ref.dtype)
    out_ref[rank:] = parts[1].astype(out_ref.dtype)


def own_kernel(coefficients_ref, transfer_ref, own_ref, *sent_refs, level, sent_level):
    put(own_ref, complex_product(half_of(transfer_ref, level, True), coefficients_ref[...]))
    for sent_ref in sent_refs:
        sent_ref[...] = half_of(transfer_ref, sent_level, False)


def partner_kernel(own_ref, partner_ref, transfer_ref, out_ref, *, level):
    rank = transfer_ref.shape[2]
    real, imag = complex_product(half_of(transfer_ref, level, False), partner_ref[...])
    put(out_ref, (own_ref[:rank] + real, own_ref[rank:] + imag))


def both_kernel(coefficients_ref, foreign_ref, transfer_ref, own_ref, cross_ref, *, level):
    coefficients = coefficients_ref[...]
    put(own_ref, complex_product(half_of(transfer_ref, level, True), coefficients))
    put(cross_ref, complex_product(foreign_ref[...], coefficients))


def small_call(kernel, name, out_shape, *operands):
    return pl.pallas_call(
        kernel,
        in_specs=[pl.BlockSpec(memory_space=pltpu.VMEM)] * len(operands),
        out_specs=jax.tree.map(lambda _: pl.BlockSpec(memory_space=pltpu.VMEM), out_shape),
        out_shape=out_shape,
        compiler_params=pltpu.CompilerParams(vmem_limit_bytes=8 << 20),
        cost_estimate=pl.CostEstimate(flops=1 << 26, bytes_accessed=1 << 19, transcendentals=0),
        name=name,
    )(*operands)


def per_device(excitation, point_order, projection, transfer, expansion):
    coefficients = leaf_coefficients(excitation, point_order, projection)
    levels, _, rank, _ = transfer.shape
    last = levels - 1
    shape = coefficients.shape
    node = jax.ShapeDtypeStruct(shape, jnp.bfloat16)
    for level in range(last):
        partner = swap(coefficients, "leaf", 1 << level)
        out_shape = [jax.ShapeDtypeStruct(shape, jnp.float32)]
        if level == 1:
            out_shape.append(jax.ShapeDtypeStruct((2, rank, rank), jnp.bfloat16))
        own_term, *sent = small_call(
            functools.partial(own_kernel, level=level, sent_level=last),
            "own", out_shape, coefficients, transfer,
        )
        if sent:
            foreign = swap(sent[0], "leaf", 1 << last)
        coefficients = small_call(
            functools.partial(partner_kernel, level=level),
            "partner", node, own_term, partner, transfer,
        )
    own, cross = small_call(
        functools.partial(both_kernel, level=last), "both", [node, node],
        coefficients, foreign, transfer,
    )
    leaf_count = lax.axis_size("leaf")
    around = [
        swap(own, "panel", 1),
        swap(cross, "leaf", 1 << last),
        swap(cross, ("panel", "leaf"), leaf_count | 1 << last),
    ]
    total = own.astype(jnp.float32)
    for term in around:
        total = total + term.astype(jnp.float32)
    total = total.astype(jnp.bfloat16)
    across = [swap(total, "panel", mask) for mask in (4, 2, 6)]
    total = total.astype(jnp.float32)
    for term in across:
        total = total + term.astype(jnp.float32)
    total = total.astype(jnp.bfloat16)
    return expanded(total, expansion)


def solution(mesh):
    in_specs = (
        P(None, None, ("panel", "leaf")),
        P(("panel", "leaf"), None),
        P(None, None, ("panel", "leaf")),
        P(None, None, ("panel", "leaf"), None),
        P(None, None, ("panel", "leaf")),
    )
    out_specs = P(None, None, ("panel", "leaf"))
    return jax.shard_map(
        per_device, mesh=mesh, in_specs=in_specs, out_specs=out_specs, check_vma=False
    )
```

```python
import functools

import jax
import jax.numpy as jnp
from jax import lax
from jax.experimental import pallas as pl
from jax.experimental.pallas import tpu as pltpu
from jax.sharding import PartitionSpec as P


def swap(block, axis, mask):
    count = lax.axis_size(axis)
    return lax.ppermute(block, axis, [(place, place ^ mask) for place in range(count)])


def put(out_ref, parts):
    rank = out_ref.shape[0] // 2
    out_ref[:rank] = parts[0].astype(out_ref.dtype)
    out_ref[rank:] = parts[1].astype(out_ref.dtype)


def leaf_kernel(
    order_hbm, source_hbm, basis_hbm, out_ref, order_ref, row_ref, source_ref, basis_ref,
    by_point_ref, *rest,
):
    ordered_refs, (order_done, row_done, source_done, basis_done) = rest[:-4], rest[-4:]
    _, width, points = source_ref.shape
    rank = basis_ref.shape[1]
    chunk = ordered_refs[0].shape[0] // 2
    piece = points // (source_done.shape[0] // 2)
    order_copy = pltpu.make_async_copy(order_hbm, order_ref, order_done)
    row_copy = pltpu.make_async_copy(order_ref, row_ref, row_done)
    source_copies = []
    for start in range(0, points, piece):
        for part in range(2):
            here = (part, slice(None), pl.ds(start, piece))
            source_copies.append((
                part, start,
                pltpu.make_async_copy(
                    source_hbm.at[here], source_ref.at[here], source_done.at[len(source_copies)]
                ),
            ))
    basis_copies = []
    for at in range(len(ordered_refs)):
        here = (slice(None), slice(None), pl.ds(at * chunk, chunk))
        basis_copies.append(
            pltpu.make_async_copy(basis_hbm.at[here], basis_ref.at[here], basis_done.at[at])
        )
    order_copy.start()
    for _, _, copy in source_copies:
        copy.start()
    order_copy.wait()
    order_ref[...] = 2 * order_ref[...]
    row_copy.start()
    for which, (part, first, copy) in enumerate(source_copies):
        copy.wait()
        if which == 1:
            for later in basis_copies:
                later.start()
        for start in range(first, first + piece, 256):
            block = source_ref[part, :, start : start + 256].astype(jnp.float32)
            by_point_ref[pl.ds(2 * start + part, 256, stride=2), :] = block.T
    row_copy.wait()
    total = None
    for at in range(len(ordered_refs) + 1):
        if at > 0:
            basis_copies[at - 1].wait()
        if at < len(ordered_refs):
            for row in range(chunk):
                point = pl.multiple_of(row_ref[0, at * chunk + row], 2)
                ordered_refs[at][2 * row : 2 * row + 2, :] = by_point_ref[pl.ds(point, 2), :]
        if at > 0:
            ordered = jnp.concatenate(
                [
                    ordered_refs[at - 1][pl.ds(part, chunk, stride=2), :].astype(jnp.bfloat16)
                    for part in range(2)
                ],
                axis=1,
            )
            basis = basis_ref[:, :, (at - 1) * chunk : at * chunk].reshape(2 * rank, chunk)
            term = jnp.dot(basis, ordered, preferred_element_type=jnp.float32)
            total = term if total is None else total + term
    put(
        out_ref,
        (total[:rank, :width] - total[rank:, width:], total[:rank, width:] + total[rank:, :width]),
    )


def leaf_coefficients(excitation, point_order, projection, chunk=512, pieces=2):
    _, width, points = excitation.shape
    rank = projection.shape[1]
    point_order, excitation, projection = (
        pltpu.with_memory_space_constraint(array, pltpu.HBM)
        for array in (point_order, excitation, projection)
    )
    return pl.pallas_call(
        leaf_kernel,
        in_specs=[pl.BlockSpec(memory_space=pltpu.HBM)] * 3,
        out_specs=pl.BlockSpec(memory_space=pltpu.VMEM),
        out_shape=jax.ShapeDtypeStruct((2 * rank, width), jnp.bfloat16),
        scratch_shapes=[
            pltpu.VMEM((1, points), jnp.int32),
            pltpu.SMEM((1, points), jnp.int32),
            pltpu.VMEM(excitation.shape, jnp.bfloat16),
            pltpu.VMEM(projection.shape, jnp.bfloat16),
            pltpu.VMEM((2 * points, width), jnp.float32),
            *[pltpu.VMEM((2 * chunk, width), jnp.float32)] * (points // chunk),
            pltpu.SemaphoreType.DMA,
            pltpu.SemaphoreType.DMA,
            pltpu.SemaphoreType.DMA((2 * pieces,)),
            pltpu.SemaphoreType.DMA((points // chunk,)),
        ],
        compiler_params=pltpu.CompilerParams(vmem_limit_bytes=24 << 20),
        name="leaf",
    )(point_order, excitation, projection)


def expand_kernel(*refs):
    *term_refs, basis_ref, out_hbm, left_ref, out_ref, done = refs
    rank, points = basis_ref.shape[1:]
    width = term_refs[0].shape[1]
    chunk = points // done.shape[0]
    total = sum(ref[...].astype(jnp.float32) for ref in term_refs).astype(jnp.bfloat16)
    real, imag = total[:rank].T, total[rank:].T
    left_ref[:width, :rank] = real
    left_ref[:width, rank:] = -imag
    left_ref[width:, :rank] = imag
    left_ref[width:, rank:] = real
    left = left_ref[...]
    copies = []
    for at in range(points // chunk):
        here = pl.ds(at * chunk, chunk)
        basis = basis_ref[:, :, here].reshape(2 * rank, chunk)
        term = jnp.dot(left, basis, preferred_element_type=jnp.float32)
        out_ref[:, :, here] = term.reshape(2, width, chunk).astype(jnp.bfloat16)
        copies.append(
            pltpu.make_async_copy(out_ref.at[:, :, here], out_hbm.at[:, :, here], done.at[at])
        )
        copies[-1].start()
    for copy in copies:
        copy.wait()


def expanded(terms, expansion, chunk=512):
    _, rank, points = expansion.shape
    width = terms[0].shape[1]
    return pl.pallas_call(
        expand_kernel,
        in_specs=[pl.BlockSpec(memory_space=pltpu.VMEM)] * (len(terms) + 1),
        out_specs=pl.BlockSpec(memory_space=pltpu.HBM),
        out_shape=jax.ShapeDtypeStruct((2, width, points), jnp.bfloat16),
        scratch_shapes=[
            pltpu.VMEM((2 * width, 2 * rank), jnp.bfloat16),
            pltpu.VMEM((2, width, points), jnp.bfloat16),
            pltpu.SemaphoreType.DMA((points // chunk,)),
        ],
        compiler_params=pltpu.CompilerParams(vmem_limit_bytes=16 << 20),
        name="expand",
    )(*terms, expansion)


def half_of(transfer_ref, level, own):
    rank = transfer_ref.shape[2]
    upper = lax.axis_index("leaf") >> level & 1
    side = upper if own else 1 - upper
    return transfer_ref[level, :, :, pl.ds(pl.multiple_of(side * rank, rank), rank)]


def complex_product(matrix, coefficients):
    _, rows, rank = matrix.shape
    width = coefficients.shape[1]
    side_by_side = jnp.concatenate((coefficients[:rank], coefficients[rank:]), axis=1)
    term = jnp.dot(
        matrix.reshape(2 * rows, rank), side_by_side, preferred_element_type=jnp.float32
    )
    return term[:rows, :width] - term[rows:, width:], term[:rows, width:] + term[rows:, :width]


def own_kernel(coefficients_ref, transfer_ref, own_ref, *sent_refs, level, sent_level):
    put(own_ref, complex_product(half_of(transfer_ref, level, True), coefficients_ref[...]))
    for sent_ref in sent_refs:
        sent_ref[...] = half_of(transfer_ref, sent_level, False)


def partner_kernel(own_ref, partner_ref, transfer_ref, out_ref, *, level):
    rank = transfer_ref.shape[2]
    real, imag = complex_product(half_of(transfer_ref, level, False), partner_ref[...])
    put(out_ref, (own_ref[:rank] + real, own_ref[rank:] + imag))


def last_kernel(own_term_ref, partner_ref, foreign_ref, transfer_ref, own_ref, cross_ref):
    levels, _, rank, _ = transfer_ref.shape
    last = levels - 1
    real, imag = complex_product(half_of(transfer_ref, last - 1, False), partner_ref[...])
    coefficients = jnp.concatenate(
        (
            (own_term_ref[:rank] + real).astype(jnp.bfloat16),
            (own_term_ref[rank:] + imag).astype(jnp.bfloat16),
        )
    )
    put(own_ref, complex_product(half_of(transfer_ref, last, True), coefficients))
    put(cross_ref, complex_product(foreign_ref[...], coefficients))


def small_call(kernel, name, out_shape, *operands):
    return pl.pallas_call(
        kernel,
        in_specs=[pl.BlockSpec(memory_space=pltpu.VMEM)] * len(operands),
        out_specs=jax.tree.map(lambda _: pl.BlockSpec(memory_space=pltpu.VMEM), out_shape),
        out_shape=out_shape,
        compiler_params=pltpu.CompilerParams(vmem_limit_bytes=8 << 20),
        cost_estimate=pl.CostEstimate(flops=1 << 26, bytes_accessed=1 << 19, transcendentals=0),
        name=name,
    )(*operands)


def per_device(excitation, point_order, projection, transfer, expansion):
    coefficients = leaf_coefficients(excitation, point_order, projection)
    levels, _, rank, _ = transfer.shape
    last = levels - 1
    shape = coefficients.shape
    node = jax.ShapeDtypeStruct(shape, jnp.bfloat16)
    for level in range(last):
        partner = swap(coefficients, "leaf", 1 << level)
        out_shape = [jax.ShapeDtypeStruct(shape, jnp.float32)]
        if level == 1:
            out_shape.append(jax.ShapeDtypeStruct((2, rank, rank), jnp.bfloat16))
        own_term, *sent = small_call(
            functools.partial(own_kernel, level=level, sent_level=last),
            "own", out_shape, coefficients, transfer,
        )
        if sent:
            foreign = swap(sent[0], "leaf", 1 << last)
        if level < last - 1:
            coefficients = small_call(
                functools.partial(partner_kernel, level=level),
                "partner", node, own_term, partner, transfer,
            )
    own, cross = small_call(
        last_kernel, "last", [node, node], own_term, partner, foreign, transfer
    )
    leaf_count = lax.axis_size("leaf")
    around = [
        swap(own, "panel", 1),
        swap(cross, "leaf", 1 << last),
        swap(cross, ("panel", "leaf"), leaf_count | 1 << last),
    ]
    total = own.astype(jnp.float32)
    for term in around:
        total = total + term.astype(jnp.float32)
    total = total.astype(jnp.bfloat16)
    across = [swap(total, "panel", mask) for mask in (2, 4, 6)]
    return expanded((total, *across), expansion)


def solution(mesh):
    in_specs = (
        P(None, None, ("panel", "leaf")),
        P(("panel", "leaf"), None),
        P(None, None, ("panel", "leaf")),
        P(None, None, ("panel", "leaf"), None),
        P(None, None, ("panel", "leaf")),
    )
    out_specs = P(None, None, ("panel", "leaf"))
    return jax.shard_map(
        per_device, mesh=mesh, in_specs=in_specs, out_specs=out_specs, check_vma=False
    )
```

```python
import functools

import jax
import jax.numpy as jnp
from jax import lax
from jax.experimental import pallas as pl
from jax.experimental.pallas import tpu as pltpu
from jax.sharding import PartitionSpec as P


def swap(block, axis, mask):
    count = lax.axis_size(axis)
    return lax.ppermute(block, axis, [(place, place ^ mask) for place in range(count)])


def put(out_ref, parts):
    rank = out_ref.shape[0] // 2
    out_ref[:rank] = parts[0].astype(out_ref.dtype)
    out_ref[rank:] = parts[1].astype(out_ref.dtype)


def leaf_kernel(
    order_hbm, source_hbm, basis_hbm, transfer_hbm, out_ref, transfer_ref, order_ref, row_ref,
    source_ref, basis_ref, by_point_ref, *rest,
):
    ordered_refs, rest = rest[:-5], rest[-5:]
    order_done, row_done, source_done, basis_done, transfer_done = rest
    _, width, points = source_ref.shape
    rank = basis_ref.shape[1]
    chunk = ordered_refs[0].shape[0] // 2
    piece = points // (source_done.shape[0] // 2)
    order_copy = pltpu.make_async_copy(order_hbm, order_ref, order_done)
    row_copy = pltpu.make_async_copy(order_ref, row_ref, row_done)
    source_copies = []
    for start in range(0, points, piece):
        for part in range(2):
            here = (part, slice(None), pl.ds(start, piece))
            source_copies.append((
                part, start,
                pltpu.make_async_copy(
                    source_hbm.at[here], source_ref.at[here], source_done.at[len(source_copies)]
                ),
            ))
    basis_copies = []
    for at in range(len(ordered_refs)):
        here = (slice(None), slice(None), pl.ds(at * chunk, chunk))
        basis_copies.append(
            pltpu.make_async_copy(basis_hbm.at[here], basis_ref.at[here], basis_done.at[at])
        )
    transfer_copy = pltpu.make_async_copy(transfer_hbm, transfer_ref, transfer_done)
    order_copy.start()
    for _, _, copy in source_copies:
        copy.start()
    for copy in basis_copies[:1]:
        copy.start()
    order_copy.wait()
    for copy in basis_copies[1:]:
        copy.start()
    order_ref[...] = 2 * order_ref[...]
    row_copy.start()
    for part, first, copy in source_copies:
        copy.wait()
        for start in range(first, first + piece, 256):
            block = source_ref[part, :, start : start + 256].astype(jnp.float32)
            by_point_ref[pl.ds(2 * start + part, 256, stride=2), :] = block.T
    row_copy.wait()
    transfer_copy.start()
    total = None
    for at in range(len(ordered_refs) + 1):
        if at > 0:
            basis_copies[at - 1].wait()
        if at < len(ordered_refs):
            for row in range(chunk):
                point = pl.multiple_of(row_ref[0, at * chunk + row], 2)
                ordered_refs[at][2 * row : 2 * row + 2, :] = by_point_ref[pl.ds(point, 2), :]
        if at > 0:
            ordered = jnp.concatenate(
                [
                    ordered_refs[at - 1][pl.ds(part, chunk, stride=2), :].astype(jnp.bfloat16)
                    for part in range(2)
                ],
                axis=1,
            )
            basis = basis_ref[:, :, (at - 1) * chunk : at * chunk].reshape(2 * rank, chunk)
            term = jnp.dot(basis, ordered, preferred_element_type=jnp.float32)
            total = term if total is None else total + term
    transfer_copy.wait()
    put(
        out_ref,
        (total[:rank, :width] - total[rank:, width:], total[:rank, width:] + total[rank:, :width]),
    )


def leaf_coefficients(excitation, point_order, projection, transfer, chunk=512, pieces=1):
    _, width, points = excitation.shape
    rank = projection.shape[1]
    operands = [
        pltpu.with_memory_space_constraint(array, pltpu.HBM)
        for array in (point_order, excitation, projection, transfer)
    ]
    return pl.pallas_call(
        leaf_kernel,
        in_specs=[pl.BlockSpec(memory_space=pltpu.HBM)] * len(operands),
        out_specs=[pl.BlockSpec(memory_space=pltpu.VMEM)] * 2,
        out_shape=[
            jax.ShapeDtypeStruct((2 * rank, width), jnp.bfloat16),
            jax.ShapeDtypeStruct(transfer.shape, jnp.bfloat16),
        ],
        scratch_shapes=[
            pltpu.VMEM((1, points), jnp.int32),
            pltpu.SMEM((1, points), jnp.int32),
            pltpu.VMEM(excitation.shape, jnp.bfloat16),
            pltpu.VMEM(projection.shape, jnp.bfloat16),
            pltpu.VMEM((2 * points, width), jnp.float32),
            *[pltpu.VMEM((2 * chunk, width), jnp.float32)] * (points // chunk),
            pltpu.SemaphoreType.DMA,
            pltpu.SemaphoreType.DMA,
            pltpu.SemaphoreType.DMA((2 * pieces,)),
            pltpu.SemaphoreType.DMA((points // chunk,)),
            pltpu.SemaphoreType.DMA,
        ],
        compiler_params=pltpu.CompilerParams(vmem_limit_bytes=24 << 20),
        name="leaf",
    )(*operands)


def expand_kernel(*refs):
    *term_refs, basis_ref, out_hbm, left_ref, out_ref, done = refs
    rank, points = basis_ref.shape[1:]
    width = term_refs[0].shape[1]
    chunk = points // done.shape[0]
    total = sum(ref[...].astype(jnp.float32) for ref in term_refs).astype(jnp.bfloat16)
    real, imag = total[:rank].T, total[rank:].T
    left_ref[:width, :rank] = real
    left_ref[:width, rank:] = -imag
    left_ref[width:, :rank] = imag
    left_ref[width:, rank:] = real
    left = left_ref[...]
    copies = []
    for at in range(points // chunk):
        here = pl.ds(at * chunk, chunk)
        basis = basis_ref[:, :, here].reshape(2 * rank, chunk)
        term = jnp.dot(left, basis, preferred_element_type=jnp.float32)
        out_ref[:, :, here] = term.reshape(2, width, chunk).astype(jnp.bfloat16)
        copies.append(
            pltpu.make_async_copy(out_ref.at[:, :, here], out_hbm.at[:, :, here], done.at[at])
        )
        copies[-1].start()
    for copy in copies:
        copy.wait()


def expanded(terms, expansion, chunk=512):
    _, rank, points = expansion.shape
    width = terms[0].shape[1]
    return pl.pallas_call(
        expand_kernel,
        in_specs=[pl.BlockSpec(memory_space=pltpu.VMEM)] * (len(terms) + 1),
        out_specs=pl.BlockSpec(memory_space=pltpu.HBM),
        out_shape=jax.ShapeDtypeStruct((2, width, points), jnp.bfloat16),
        scratch_shapes=[
            pltpu.VMEM((2 * width, 2 * rank), jnp.bfloat16),
            pltpu.VMEM((2, width, points), jnp.bfloat16),
            pltpu.SemaphoreType.DMA((points // chunk,)),
        ],
        compiler_params=pltpu.CompilerParams(vmem_limit_bytes=16 << 20),
        name="expand",
    )(*terms, expansion)


def half_of(transfer_ref, level, own):
    rank = transfer_ref.shape[2]
    upper = lax.axis_index("leaf") >> level & 1
    side = upper if own else 1 - upper
    return transfer_ref[level, :, :, pl.ds(pl.multiple_of(side * rank, rank), rank)]


def complex_product(matrix, coefficients):
    _, rows, rank = matrix.shape
    width = coefficients.shape[1]
    side_by_side = jnp.concatenate((coefficients[:rank], coefficients[rank:]), axis=1)
    term = jnp.dot(
        matrix.reshape(2 * rows, rank), side_by_side, preferred_element_type=jnp.float32
    )
    return term[:rows, :width] - term[rows:, width:], term[:rows, width:] + term[rows:, :width]


def own_kernel(coefficients_ref, transfer_ref, own_ref, *sent_refs, level, sent_level):
    put(own_ref, complex_product(half_of(transfer_ref, level, True), coefficients_ref[...]))
    for sent_ref in sent_refs:
        sent_ref[...] = half_of(transfer_ref, sent_level, False)


def partner_kernel(own_ref, partner_ref, transfer_ref, out_ref, *, level):
    rank = transfer_ref.shape[2]
    real, imag = complex_product(half_of(transfer_ref, level, False), partner_ref[...])
    put(out_ref, (own_ref[:rank] + real, own_ref[rank:] + imag))


def last_kernel(own_term_ref, partner_ref, foreign_ref, transfer_ref, own_ref, cross_ref):
    levels, _, rank, _ = transfer_ref.shape
    last = levels - 1
    real, imag = complex_product(half_of(transfer_ref, last - 1, False), partner_ref[...])
    coefficients = jnp.concatenate(
        (
            (own_term_ref[:rank] + real).astype(jnp.bfloat16),
            (own_term_ref[rank:] + imag).astype(jnp.bfloat16),
        )
    )
    put(own_ref, complex_product(half_of(transfer_ref, last, True), coefficients))
    put(cross_ref, complex_product(foreign_ref[...], coefficients))


def small_call(kernel, name, out_shape, *operands):
    return pl.pallas_call(
        kernel,
        in_specs=[pl.BlockSpec(memory_space=pltpu.VMEM)] * len(operands),
        out_specs=jax.tree.map(lambda _: pl.BlockSpec(memory_space=pltpu.VMEM), out_shape),
        out_shape=out_shape,
        compiler_params=pltpu.CompilerParams(vmem_limit_bytes=8 << 20),
        cost_estimate=pl.CostEstimate(flops=1 << 26, bytes_accessed=1 << 19, transcendentals=0),
        name=name,
    )(*operands)


def per_device(excitation, point_order, projection, transfer, expansion):
    coefficients, transfer = leaf_coefficients(excitation, point_order, projection, transfer)
    levels, _, rank, _ = transfer.shape
    last = levels - 1
    shape = coefficients.shape
    node = jax.ShapeDtypeStruct(shape, jnp.bfloat16)
    for level in range(last):
        partner = swap(coefficients, "leaf", 1 << level)
        out_shape = [jax.ShapeDtypeStruct(shape, jnp.float32)]
        if level == 1:
            out_shape.append(jax.ShapeDtypeStruct((2, rank, rank), jnp.bfloat16))
        own_term, *sent = small_call(
            functools.partial(own_kernel, level=level, sent_level=last),
            "own", out_shape, coefficients, transfer,
        )
        if sent:
            foreign = swap(sent[0], "leaf", 1 << last)
        if level < last - 1:
            coefficients = small_call(
                functools.partial(partner_kernel, level=level),
                "partner", node, own_term, partner, transfer,
            )
    own, cross = small_call(
        last_kernel, "last", [node, node], own_term, partner, foreign, transfer
    )
    leaf_count = lax.axis_size("leaf")
    around = [
        swap(own, "panel", 1),
        swap(cross, "leaf", 1 << last),
        swap(cross, ("panel", "leaf"), leaf_count | 1 << last),
    ]
    total = own.astype(jnp.float32)
    for term in around:
        total = total + term.astype(jnp.float32)
    total = total.astype(jnp.bfloat16)
    across = [swap(total, "panel", mask) for mask in (2, 4, 6)]
    return expanded((total, *across), expansion)


def solution(mesh):
    in_specs = (
        P(None, None, ("panel", "leaf")),
        P(("panel", "leaf"), None),
        P(None, None, ("panel", "leaf")),
        P(None, None, ("panel", "leaf"), None),
        P(None, None, ("panel", "leaf")),
    )
    out_specs = P(None, None, ("panel", "leaf"))
    return jax.shard_map(
        per_device, mesh=mesh, in_specs=in_specs, out_specs=out_specs, check_vma=False
    )
```

```python
import functools

import jax
import jax.numpy as jnp
from jax import lax
from jax.experimental import pallas as pl
from jax.experimental.pallas import tpu as pltpu
from jax.sharding import PartitionSpec as P


def swap(block, axis, mask):
    count = lax.axis_size(axis)
    return lax.ppermute(block, axis, [(place, place ^ mask) for place in range(count)])


def put(out_ref, parts):
    rank = out_ref.shape[0] // 2
    out_ref[:rank] = parts[0].astype(out_ref.dtype)
    out_ref[rank:] = parts[1].astype(out_ref.dtype)


def leaf_kernel(
    order_hbm, source_hbm, basis_hbm, transfer_hbm, out_ref, transfer_ref, order_ref, row_ref,
    source_ref, basis_ref, by_point_ref, *rest,
):
    ordered_refs, rest = rest[:-5], rest[-5:]
    order_done, row_done, source_done, basis_done, transfer_done = rest
    _, width, points = source_ref.shape
    rank = basis_ref.shape[1]
    chunk = ordered_refs[0].shape[0] // 2
    piece = points // (source_done.shape[0] // 2)
    order_copy = pltpu.make_async_copy(order_hbm, order_ref, order_done)
    row_copy = pltpu.make_async_copy(order_ref, row_ref, row_done)
    source_copies = []
    for start in range(0, points, piece):
        for part in range(2):
            here = (part, slice(None), pl.ds(start, piece))
            source_copies.append((
                part, start,
                pltpu.make_async_copy(
                    source_hbm.at[here], source_ref.at[here], source_done.at[len(source_copies)]
                ),
            ))
    basis_copies = []
    for at in range(len(ordered_refs)):
        here = (slice(None), slice(None), pl.ds(at * chunk, chunk))
        basis_copies.append(
            pltpu.make_async_copy(basis_hbm.at[here], basis_ref.at[here], basis_done.at[at])
        )
    transfer_copy = pltpu.make_async_copy(transfer_hbm, transfer_ref, transfer_done)
    order_copy.start()
    for _, _, copy in source_copies:
        copy.start()
    for copy in basis_copies[:1]:
        copy.start()
    order_copy.wait()
    for copy in basis_copies[1:]:
        copy.start()
    order_ref[...] = 2 * order_ref[...]
    row_copy.start()
    for part, first, copy in source_copies:
        copy.wait()
        for start in range(first, first + piece, 256):
            block = source_ref[part, :, start : start + 256].astype(jnp.float32)
            by_point_ref[pl.ds(2 * start + part, 256, stride=2), :] = block.T
    row_copy.wait()
    transfer_copy.start()
    total = None
    for at in range(len(ordered_refs) + 1):
        if at > 0:
            basis_copies[at - 1].wait()
        if at < len(ordered_refs):
            for row in range(chunk):
                point = pl.multiple_of(row_ref[0, at * chunk + row], 2)
                ordered_refs[at][2 * row : 2 * row + 2, :] = by_point_ref[pl.ds(point, 2), :]
        if at > 0:
            ordered = jnp.concatenate(
                [
                    ordered_refs[at - 1][pl.ds(part, chunk, stride=2), :].astype(jnp.bfloat16)
                    for part in range(2)
                ],
                axis=1,
            )
            basis = basis_ref[:, :, (at - 1) * chunk : at * chunk].reshape(2 * rank, chunk)
            term = jnp.dot(basis, ordered, preferred_element_type=jnp.float32)
            total = term if total is None else total + term
    transfer_copy.wait()
    put(
        out_ref,
        (total[:rank, :width] - total[rank:, width:], total[:rank, width:] + total[rank:, :width]),
    )


def leaf_coefficients(excitation, point_order, projection, transfer, chunk=512, pieces=1):
    _, width, points = excitation.shape
    rank = projection.shape[1]
    operands = [
        pltpu.with_memory_space_constraint(array, pltpu.HBM)
        for array in (point_order, excitation, projection, transfer)
    ]
    return pl.pallas_call(
        leaf_kernel,
        in_specs=[pl.BlockSpec(memory_space=pltpu.HBM)] * len(operands),
        out_specs=[pl.BlockSpec(memory_space=pltpu.VMEM)] * 2,
        out_shape=[
            jax.ShapeDtypeStruct((2 * rank, width), jnp.bfloat16),
            jax.ShapeDtypeStruct(transfer.shape, jnp.bfloat16),
        ],
        scratch_shapes=[
            pltpu.VMEM((1, points), jnp.int32),
            pltpu.SMEM((1, points), jnp.int32),
            pltpu.VMEM(excitation.shape, jnp.bfloat16),
            pltpu.VMEM(projection.shape, jnp.bfloat16),
            pltpu.VMEM((2 * points, width), jnp.float32),
            *[pltpu.VMEM((2 * chunk, width), jnp.float32)] * (points // chunk),
            pltpu.SemaphoreType.DMA,
            pltpu.SemaphoreType.DMA,
            pltpu.SemaphoreType.DMA((2 * pieces,)),
            pltpu.SemaphoreType.DMA((points // chunk,)),
            pltpu.SemaphoreType.DMA,
        ],
        compiler_params=pltpu.CompilerParams(vmem_limit_bytes=24 << 20),
        name="leaf",
    )(*operands)


def expand_kernel(*refs):
    *term_refs, basis_ref, out_hbm, left_ref, out_ref, done = refs
    rank, points = basis_ref.shape[1:]
    width = term_refs[0].shape[1]
    chunk = points // done.shape[0]
    total = sum(ref[...].astype(jnp.float32) for ref in term_refs).astype(jnp.bfloat16)
    real, imag = total[:rank].T, total[rank:].T
    left_ref[:width, :rank] = real
    left_ref[:width, rank:] = -imag
    left_ref[width:, :rank] = imag
    left_ref[width:, rank:] = real
    left = left_ref[...]
    copies = []
    for at in range(points // chunk):
        here = pl.ds(at * chunk, chunk)
        basis = basis_ref[:, :, here].reshape(2 * rank, chunk)
        term = jnp.dot(left, basis, preferred_element_type=jnp.float32)
        out_ref[:, :, here] = term.reshape(2, width, chunk).astype(jnp.bfloat16)
        copies.append(
            pltpu.make_async_copy(out_ref.at[:, :, here], out_hbm.at[:, :, here], done.at[at])
        )
        copies[-1].start()
    for copy in copies:
        copy.wait()


def expanded(terms, expansion, chunk=256):
    _, rank, points = expansion.shape
    width = terms[0].shape[1]
    return pl.pallas_call(
        expand_kernel,
        in_specs=[pl.BlockSpec(memory_space=pltpu.VMEM)] * (len(terms) + 1),
        out_specs=pl.BlockSpec(memory_space=pltpu.HBM),
        out_shape=jax.ShapeDtypeStruct((2, width, points), jnp.bfloat16),
        scratch_shapes=[
            pltpu.VMEM((2 * width, 2 * rank), jnp.bfloat16),
            pltpu.VMEM((2, width, points), jnp.bfloat16),
            pltpu.SemaphoreType.DMA((points // chunk,)),
        ],
        compiler_params=pltpu.CompilerParams(vmem_limit_bytes=16 << 20),
        name="expand",
    )(*terms, expansion)


def half_of(transfer_ref, level, own):
    rank = transfer_ref.shape[2]
    upper = lax.axis_index("leaf") >> level & 1
    side = upper if own else 1 - upper
    return transfer_ref[level, :, :, pl.ds(pl.multiple_of(side * rank, rank), rank)]


def complex_product(matrix, coefficients):
    _, rows, rank = matrix.shape
    width = coefficients.shape[1]
    side_by_side = jnp.concatenate((coefficients[:rank], coefficients[rank:]), axis=1)
    term = jnp.dot(
        matrix.reshape(2 * rows, rank), side_by_side, preferred_element_type=jnp.float32
    )
    return term[:rows, :width] - term[rows:, width:], term[:rows, width:] + term[rows:, :width]


def own_kernel(coefficients_ref, transfer_ref, own_ref, *sent_refs, level, sent_level):
    put(own_ref, complex_product(half_of(transfer_ref, level, True), coefficients_ref[...]))
    for sent_ref in sent_refs:
        sent_ref[...] = half_of(transfer_ref, sent_level, False)


def partner_kernel(own_ref, partner_ref, transfer_ref, out_ref, *, level):
    rank = transfer_ref.shape[2]
    real, imag = complex_product(half_of(transfer_ref, level, False), partner_ref[...])
    put(out_ref, (own_ref[:rank] + real, own_ref[rank:] + imag))


def last_kernel(own_term_ref, partner_ref, foreign_ref, transfer_ref, own_ref, cross_ref):
    levels, _, rank, _ = transfer_ref.shape
    last = levels - 1
    real, imag = complex_product(half_of(transfer_ref, last - 1, False), partner_ref[...])
    coefficients = jnp.concatenate(
        (
            (own_term_ref[:rank] + real).astype(jnp.bfloat16),
            (own_term_ref[rank:] + imag).astype(jnp.bfloat16),
        )
    )
    put(own_ref, complex_product(half_of(transfer_ref, last, True), coefficients))
    put(cross_ref, complex_product(foreign_ref[...], coefficients))


def small_call(kernel, name, out_shape, *operands):
    return pl.pallas_call(
        kernel,
        in_specs=[pl.BlockSpec(memory_space=pltpu.VMEM)] * len(operands),
        out_specs=jax.tree.map(lambda _: pl.BlockSpec(memory_space=pltpu.VMEM), out_shape),
        out_shape=out_shape,
        compiler_params=pltpu.CompilerParams(vmem_limit_bytes=8 << 20),
        cost_estimate=pl.CostEstimate(flops=1 << 26, bytes_accessed=1 << 19, transcendentals=0),
        name=name,
    )(*operands)


def per_device(excitation, point_order, projection, transfer, expansion):
    coefficients, transfer = leaf_coefficients(excitation, point_order, projection, transfer)
    levels, _, rank, _ = transfer.shape
    last = levels - 1
    shape = coefficients.shape
    node = jax.ShapeDtypeStruct(shape, jnp.bfloat16)
    for level in range(last):
        partner = swap(coefficients, "leaf", 1 << level)
        out_shape = [jax.ShapeDtypeStruct(shape, jnp.float32)]
        if level == 1:
            out_shape.append(jax.ShapeDtypeStruct((2, rank, rank), jnp.bfloat16))
        own_term, *sent = small_call(
            functools.partial(own_kernel, level=level, sent_level=last),
            "own", out_shape, coefficients, transfer,
        )
        if sent:
            foreign = swap(sent[0], "leaf", 1 << last)
        if level < last - 1:
            coefficients = small_call(
                functools.partial(partner_kernel, level=level),
                "partner", node, own_term, partner, transfer,
            )
    own, cross = small_call(
        last_kernel, "last", [node, node], own_term, partner, foreign, transfer
    )
    leaf_count = lax.axis_size("leaf")
    around = [
        swap(own, "panel", 1),
        swap(cross, "leaf", 1 << last),
        swap(cross, ("panel", "leaf"), leaf_count | 1 << last),
    ]
    total = own.astype(jnp.float32)
    for term in around:
        total = total + term.astype(jnp.float32)
    total = total.astype(jnp.bfloat16)
    across = [swap(total, "panel", mask) for mask in (2, 4, 6)]
    return expanded((total, *across), expansion)


def solution(mesh):
    in_specs = (
        P(None, None, ("panel", "leaf")),
        P(("panel", "leaf"), None),
        P(None, None, ("panel", "leaf")),
        P(None, None, ("panel", "leaf"), None),
        P(None, None, ("panel", "leaf")),
    )
    out_specs = P(None, None, ("panel", "leaf"))
    return jax.shard_map(
        per_device, mesh=mesh, in_specs=in_specs, out_specs=out_specs, check_vma=False
    )
```
